32 devices in a mesh: dp: 4 (over x, core), expert: 8 (over z, y).
Axes of the slice: x: 2, y: 2, z: 4, core: 2. Of those that a mesh axis runs over, the one named last changes fastest.
Arguments:
- tokens: bfloat16 [6304, 768], P(('dp', 'expert')), may hold values from -6 to 6
- packed_weight: bfloat16 [768, 2304], P(('dp', 'expert')), may hold values from -0.21875 to 0.21875
- output_weight: bfloat16 [768, 768], P(('dp', 'expert')), may hold values from -0.625 to 0.625
- router_weight: bfloat16 [768, 8], P(('dp', 'expert')), may hold values from -0.21875 to 0.21875
- first_gain: bfloat16 [768], P(('dp', 'expert')), may hold values from 0.5 to 1.5
- first_bias: bfloat16 [768], P(('dp', 'expert')), may hold values from -3 to 3
- second_gain: bfloat16 [768], P(('dp', 'expert')), may hold values from 0.5 to 1.5
- second_bias: bfloat16 [768], P(('dp', 'expert')), may hold values from -3 to 3
- expert_up: bfloat16 [8, 768, 3072], P('expert', None, 'dp'), may hold values from -0.21875 to 0.21875
- expert_down: bfloat16 [8, 768, 3072], P('expert', None, 'dp'), may hold values from -0.875 to 0.875
- expert_choice: int32 [6304, 2], P(('dp', 'expert')), may hold values from 0 to 7, as said below
- slot_index: int32 [6304, 2], P(('dp', 'expert')), may hold values from 0 to 46, as said below
- cotangent: bfloat16 [6304, 768], P(('dp', 'expert')), may hold values from -6 to 6
Outputs:
- block_output: bfloat16 [6304, 768], P(('dp', 'expert'))
- input_grad: bfloat16 [6304, 768], P(('dp', 'expert'))
- packed_grad: float32 [768, 2304], P(('dp', 'expert'))
- output_grad: float32 [768, 768], P(('dp', 'expert'))
- router_grad: float32 [768, 8], P(('dp', 'expert'))
- first_gain_grad: float32 [768], P(('dp', 'expert'))
- first_bias_grad: float32 [768], P(('dp', 'expert'))
- second_gain_grad: float32 [768], P(('dp', 'expert'))
- second_bias_grad: float32 [768], P(('dp', 'expert'))
- expert_up_grad: float32 [8, 768, 3072], P('expert', None, 'dp')
- expert_down_grad: float32 [8, 768, 3072], P('expert', None, 'dp')
The draws below stay inside these ranges and needn't reach their ends.
Inputs may be any that keep to these rules, and one draw needn't show every extreme that they name: `expert_choice`: each row names 2 different experts. `slot_index`: among the tokens of one device, taken choice by choice and then token by token, the number of earlier choices of the same expert, or 46 where that number is 46 or more.
All inputs are finite; a program needn't handle non-finite values.
Results may differ from the reference program's by a relative error of at most 0.019.
Values may be sent and summed in bfloat16 or wider, within the bound.
A program may use at most 128 MiB of HBM per device.

```python
import jax
import jax.numpy as jnp
from jax import lax

D = 768
HEADS = 12
HEAD = 64
FF = 3072
TOP = 2
SEQ = 197
EXPERT_TOTAL = 8
TOK_DEV = 197
TOKENS = 6304
CAP = 46
N_DP = 4
N_EXPERT = 8


def route_table(key):
    base = jax.random.fold_in(key, 11)
    initial_key, second_key = jax.random.split(base)
    extra_amount = jax.random.randint(initial_key, (EXPERT_TOTAL,), 0, 3) * 128
    random_jitter = jax.random.randint(second_key, (TOKENS, EXPERT_TOTAL), 0, 4096)
    router_scores = (random_jitter + extra_amount[None, :]) * EXPERT_TOTAL + jnp.arange(EXPERT_TOTAL, dtype=jnp.int32)[None, :]
    unused, chosen = lax.top_k(router_scores, TOP)
    chosen = chosen.astype(jnp.int32)
    blocks = TOKENS // TOK_DEV
    ordered = jnp.transpose(chosen.reshape(blocks, TOK_DEV, TOP), (0, 2, 1)).reshape(blocks, TOP * TOK_DEV)
    onehot = (ordered[:, :, None] == jnp.arange(EXPERT_TOTAL, dtype=jnp.int32)[None, None, :]).astype(jnp.int32)
    counts = jnp.cumsum(onehot, axis=1)
    ranks = jnp.sum(counts * onehot, axis=2) - 1
    slots = jnp.minimum(ranks, CAP)
    slots = jnp.transpose(slots.reshape(blocks, TOP, TOK_DEV), (0, 2, 1)).reshape(TOKENS, TOP)
    return (chosen, slots.astype(jnp.int32))


def draw_expert_choice(key, part):
    return route_table(key)[0]


def draw_slot_index(key, part):
    return route_table(key)[1]


def raised(drawn, key, source, target, shards_of, factor):
    def block_of(axis_at):
        return (jnp.arange(drawn.shape[axis_at]) // (drawn.shape[axis_at] // shards_of)).reshape((-1,) + (1,) * (drawn.ndim - 1 - axis_at))

    near = jax.random.permutation(key, shards_of)[block_of(target)]
    far = (block_of(target) + shards_of // 2) % shards_of
    return jnp.where((block_of(source) == near) | (block_of(source) == far), factor * drawn, drawn)


def steps_of(stream_key, dims, cuts, least, largest):
    gain = 1.0
    for axis_at, shards_of in cuts:
        steps = jax.random.uniform(jax.random.fold_in(jax.random.fold_in(stream_key, 6), axis_at), (shards_of,), jnp.float32, least / len(cuts), largest / len(cuts))
        gain = gain * jnp.repeat(jnp.exp(steps), dims[axis_at] // shards_of).reshape((-1,) + (1,) * (len(dims) - 1 - axis_at))
    return gain


def noise(stream_key, extent, width, limit, cuts=(), kind=jnp.bfloat16):
    gain = steps_of(stream_key, extent, cuts, -0.22, 0.18) if cuts else 1.0
    values = jax.random.normal(stream_key, extent, jnp.float32) * width * gain
    return jnp.minimum(jnp.maximum(values, -limit), limit).astype(kind)


def heavy_noise(stream_key, shape, deviation, bound, pieces, heavy, kind=jnp.bfloat16):
    values = deviation * jax.random.normal(stream_key, shape, jnp.float32)
    if pieces:
        values = values * steps_of(stream_key, shape, pieces, -0.22, 0.18)
    return jnp.clip(raised(values, jax.random.fold_in(stream_key, 3), *heavy), -bound, bound).astype(kind)


def setup_inputs(seed: int = 0) -> dict:
    arg_keys = jax.random.split(jax.random.key(seed), 14)
    return {
        "tokens": heavy_noise(arg_keys[0], (TOKENS, D), 1.0, 6.0, ((0, 32),), (0, 1, 32, 2.75)),
        "packed_weight": noise(arg_keys[1], (D, 3 * D), D ** -0.5, 0.21875, ((0, 32),)),
        "output_weight": noise(arg_keys[2], (D, D), (D // 8) ** -0.5, 0.625, ((0, 32),)),
        "router_weight": noise(arg_keys[3], (D, EXPERT_TOTAL), D ** -0.5, 0.21875, ((0, 32),)),
        "first_gain": jnp.clip(1.0 + 0.1 * jax.random.normal(arg_keys[4], (D,), jnp.float32), 0.5, 1.5).astype(jnp.bfloat16),
        "first_bias": noise(arg_keys[5], (D,), 0.5, 3.0, ((0, 32),)),
        "second_gain": jnp.clip(1.0 + 0.1 * jax.random.normal(arg_keys[6], (D,), jnp.float32), 0.5, 1.5).astype(jnp.bfloat16),
        "second_bias": noise(arg_keys[7], (D,), 0.5, 3.0, ((0, 32),)),
        "expert_up": noise(arg_keys[8], (EXPERT_TOTAL, D, FF), D ** -0.5, 0.21875, ((0, 8), (2, 4))),
        "expert_down": noise(arg_keys[9], (EXPERT_TOTAL, D, FF), (max(FF // (EXPERT_TOTAL * EXPERT_TOTAL), 1)) ** -0.5, 0.875, ((0, 8), (2, 4))),
        "expert_choice": draw_expert_choice(jax.random.fold_in(arg_keys[13], 71), 0),
        "slot_index": draw_slot_index(jax.random.fold_in(arg_keys[13], 71), 0),
        "cotangent": noise(arg_keys[12], (TOKENS, D), 1.0, 6.0, ((0, 32),)),
    }


epsilon = 1e-06
inv_root_two = 0.7071067811865476
inv_root_two_pi = 0.3989422804014327

def round_half(arg_values):
    return lax.optimization_barrier(arg_values.astype(jnp.bfloat16)).astype(jnp.float32)

def normalize(rows_in, gain_vec, offset):
    centred = rows_in - lax.optimization_barrier(jnp.mean(rows_in, axis=-1, keepdims=True))
    inverse = lax.rsqrt(lax.optimization_barrier(jnp.mean(centred * centred, axis=-1, keepdims=True)) + epsilon)
    unit_rows = centred * inverse
    return (unit_rows * gain_vec.astype(jnp.float32) + offset.astype(jnp.float32), unit_rows, inverse)

def normalize_back(grad_rows, unit_rows, inverse, gain_vec):
    grad_unit = grad_rows * gain_vec.astype(jnp.float32)
    mean_grad = lax.optimization_barrier(jnp.mean(grad_unit, axis=-1, keepdims=True))
    mean_dot = lax.optimization_barrier(jnp.mean(grad_unit * unit_rows, axis=-1, keepdims=True))
    grad_in = inverse * (grad_unit - mean_grad - unit_rows * mean_dot)
    return (grad_in, lax.optimization_barrier(jnp.sum(grad_rows * unit_rows, axis=0)), lax.optimization_barrier(jnp.sum(grad_rows, axis=0)))

def gelu_exact(arg_values):
    return 0.5 * arg_values * (1.0 + jax.scipy.special.erf(arg_values * inv_root_two))

def gelu_slope(arg_values):
    return 0.5 * (1.0 + jax.scipy.special.erf(arg_values * inv_root_two)) + arg_values * jnp.exp(-0.5 * arg_values * arg_values) * inv_root_two_pi

def attend_block(packed_heads):
    queries = packed_heads[:, :, 0].astype(jnp.float32)
    key_rows = packed_heads[:, :, 1].astype(jnp.float32)
    values = packed_heads[:, :, 2].astype(jnp.float32)
    router_scores = jnp.einsum('ishd,ithd->ihst', queries, key_rows) * HEAD ** (-0.5)
    log_total = jnp.log(lax.optimization_barrier(jnp.sum(jnp.exp(router_scores), axis=-1, keepdims=True)))
    weights = round_half(jnp.exp(router_scores - log_total))
    mixed_heads = jnp.einsum('ihst,ithd->ishd', weights, values)
    return (mixed_heads.astype(jnp.bfloat16), log_total)

def attend_back(operands):
    packed_heads, log_total, grad_mixed = operands
    queries = packed_heads[:, :, 0].astype(jnp.float32)
    key_rows = packed_heads[:, :, 1].astype(jnp.float32)
    values = packed_heads[:, :, 2].astype(jnp.float32)
    grad_heads = grad_mixed.astype(jnp.float32)
    router_scores = jnp.einsum('ishd,ithd->ihst', queries, key_rows) * HEAD ** (-0.5)
    weights = jnp.exp(router_scores - log_total)
    rounded = round_half(weights)
    grad_values = jnp.einsum('ihst,ishd->ithd', rounded, grad_heads)
    grad_weights = jnp.einsum('ishd,ithd->ihst', grad_heads, values)
    row_delta = lax.optimization_barrier(jnp.sum(weights * grad_weights, axis=-1, keepdims=True))
    grad_scores = round_half(weights * (grad_weights - row_delta) * HEAD ** (-0.5))
    grad_queries = jnp.einsum('ihst,ithd->ishd', grad_scores, key_rows)
    grad_keys = jnp.einsum('ihst,ishd->ithd', grad_scores, queries)
    return jnp.stack([grad_queries, grad_keys, grad_values], axis=2)

def expert_forward(operands):
    slot_rows, weight_up, weight_down = operands
    before_act = jnp.dot(slot_rows, weight_up, preferred_element_type=jnp.float32)
    hidden = gelu_exact(before_act).astype(jnp.bfloat16)
    return jnp.dot(hidden, weight_down.T, preferred_element_type=jnp.float32).astype(jnp.bfloat16)

def expert_backward(operands):
    slot_rows, grad_rows, weight_up, weight_down = operands
    before_act = jnp.dot(slot_rows, weight_up, preferred_element_type=jnp.float32)
    hidden = gelu_exact(before_act).astype(jnp.bfloat16)
    grad_hidden = jnp.dot(grad_rows, weight_down, preferred_element_type=jnp.float32)
    grad_pre = (grad_hidden * gelu_slope(before_act)).astype(jnp.bfloat16)
    grad_down = jnp.dot(grad_rows.T, hidden, preferred_element_type=jnp.float32)
    grad_up = jnp.dot(slot_rows.T, grad_pre, preferred_element_type=jnp.float32)
    grad_sent = jnp.dot(grad_pre, weight_up.T, preferred_element_type=jnp.float32).astype(jnp.bfloat16)
    return (grad_sent, grad_up, grad_down)

def reference(tokens, packed_weight, output_weight, router_weight, first_gain, first_bias, second_gain, second_bias, expert_up, expert_down, expert_choice, slot_index, cotangent):
    devices = N_DP * N_EXPERT
    images = TOKENS // SEQ
    blocks = N_DP
    slot_count = EXPERT_TOTAL * CAP + 1
    inputs = tokens.astype(jnp.float32)
    normed_first, unit_first, inverse_first = normalize(inputs, first_gain, first_bias)
    normed_first = normed_first.astype(jnp.bfloat16)
    packed = jnp.dot(normed_first, packed_weight, preferred_element_type=jnp.float32).astype(jnp.bfloat16)
    packed_blocks = packed.reshape(blocks, images // blocks, SEQ, 3, HEADS, HEAD)
    mixed_heads, log_total = lax.map(attend_block, packed_blocks)
    mixed_flat = mixed_heads.reshape(TOKENS, D)
    hidden_first = inputs + jnp.dot(mixed_flat, output_weight, preferred_element_type=jnp.float32)
    normed_second, unit_second, inverse_second = normalize(hidden_first, second_gain, second_bias)
    normed_second = normed_second.astype(jnp.bfloat16)
    logits = jnp.dot(normed_second, router_weight, preferred_element_type=jnp.float32)
    exp_terms = jnp.exp(logits)
    router_probs = exp_terms / lax.optimization_barrier(jnp.sum(exp_terms, axis=-1, keepdims=True))
    gate_values = jnp.take_along_axis(router_probs, expert_choice, axis=1)
    device_of = (jnp.arange(TOKENS, dtype=jnp.int32) // TOK_DEV)[:, None]
    local_slot = jnp.where(slot_index < CAP, expert_choice * CAP + slot_index, EXPERT_TOTAL * CAP)
    global_slot = (device_of * slot_count + local_slot).reshape(-1).astype(jnp.int32)

    def to_experts(slot_rows):
        slot_table = jnp.zeros((devices * slot_count, D), jnp.bfloat16).at[global_slot].set(slot_rows)
        slot_table = slot_table.reshape(devices, slot_count, D)[:, :-1].reshape(devices, EXPERT_TOTAL, CAP, D)
        return jnp.transpose(slot_table, (1, 0, 2, 3)).reshape(EXPERT_TOTAL, devices * CAP, D)

    def from_experts(slot_table):
        slot_table = jnp.transpose(slot_table.reshape(EXPERT_TOTAL, devices, CAP, D), (1, 0, 2, 3)).reshape(devices, EXPERT_TOTAL * CAP, D)
        slot_table = jnp.concatenate([slot_table, jnp.zeros((devices, 1, D), slot_table.dtype)], axis=1).reshape(devices * slot_count, D)
        return slot_table[global_slot].reshape(TOKENS, TOP, D).astype(jnp.float32)
    expert_rows = to_experts(jnp.repeat(normed_second, TOP, axis=0))
    expert_out = lax.map(expert_forward, (expert_rows, expert_up, expert_down))
    returned = from_experts(expert_out)
    combined = lax.optimization_barrier(jnp.sum(gate_values[:, :, None] * returned, axis=1))
    block_output = (hidden_first + combined).astype(jnp.bfloat16)
    grad_top = cotangent.astype(jnp.float32)
    grad_gates = lax.optimization_barrier(jnp.sum(grad_top[:, None, :] * returned, axis=2))
    grad_slots = (gate_values[:, :, None] * grad_top[:, None, :]).astype(jnp.bfloat16).reshape(TOKENS * TOP, D)
    grad_table = to_experts(grad_slots)
    grad_sent, expert_up_grad, expert_down_grad = lax.map(expert_backward, (expert_rows, grad_table, expert_up, expert_down))
    gradient_second_normed = lax.optimization_barrier(jnp.sum(from_experts(grad_sent), axis=1))
    choice_mask = (expert_choice[:, :, None] == jnp.arange(EXPERT_TOTAL, dtype=jnp.int32)[None, None, :]).astype(jnp.float32)
    grad_probs = lax.optimization_barrier(jnp.sum(choice_mask * grad_gates[:, :, None], axis=1))
    grad_logits = (router_probs * (grad_probs - lax.optimization_barrier(jnp.sum(router_probs * grad_probs, axis=1, keepdims=True)))).astype(jnp.bfloat16)
    router_grad = jnp.dot(normed_second.T, grad_logits, preferred_element_type=jnp.float32)
    gradient_second_normed = gradient_second_normed + jnp.dot(grad_logits, router_weight.T, preferred_element_type=jnp.float32)
    grad_hidden, second_gain_grad, second_bias_grad = normalize_back(gradient_second_normed, unit_second, inverse_second, second_gain)
    grad_hidden = grad_hidden + grad_top
    grad_hidden_half = grad_hidden.astype(jnp.bfloat16)
    output_grad = jnp.dot(mixed_flat.T, grad_hidden_half, preferred_element_type=jnp.float32)
    grad_mixed = jnp.dot(grad_hidden_half, output_weight.T, preferred_element_type=jnp.float32).astype(jnp.bfloat16)
    grad_mixed = grad_mixed.reshape(blocks, images // blocks, SEQ, HEADS, HEAD)
    gradient_packed_rows = lax.map(attend_back, (packed_blocks, log_total, grad_mixed))
    gradient_packed_rows = gradient_packed_rows.reshape(TOKENS, 3 * D).astype(jnp.bfloat16)
    packed_grad = jnp.dot(normed_first.T, gradient_packed_rows, preferred_element_type=jnp.float32)
    grad_normed_first = jnp.dot(gradient_packed_rows, packed_weight.T, preferred_element_type=jnp.float32)
    grad_inputs, first_gain_grad, first_bias_grad = normalize_back(grad_normed_first, unit_first, inverse_first, first_gain)
    input_grad = (grad_inputs + grad_hidden).astype(jnp.bfloat16)
    return (block_output, input_grad, packed_grad, output_grad, router_grad, first_gain_grad, first_bias_grad, second_gain_grad, second_bias_grad, expert_up_grad, expert_down_grad)
```

```python
import jax
import jax.numpy as jnp
from jax import lax
from jax.sharding import PartitionSpec as P

HEADS = 12
HEAD = 64
SEQ = 197


epsilon = 1e-06
inv_root_two = 0.7071067811865476
inv_root_two_pi = 0.3989422804014327


def normalize(rows_in, gain_vec, offset):
    centred = rows_in - jnp.mean(rows_in, axis=-1, keepdims=True)
    inverse = lax.rsqrt(jnp.mean(centred * centred, axis=-1, keepdims=True) + epsilon)
    unit_rows = centred * inverse
    return (
        unit_rows * gain_vec.astype(jnp.float32) + offset.astype(jnp.float32),
        unit_rows,
        inverse,
    )


def normalize_back(grad_rows, unit_rows, inverse, gain_vec):
    grad_unit = grad_rows * gain_vec.astype(jnp.float32)
    mean_grad = jnp.mean(grad_unit, axis=-1, keepdims=True)
    mean_dot = jnp.mean(grad_unit * unit_rows, axis=-1, keepdims=True)
    grad_in = inverse * (grad_unit - mean_grad - unit_rows * mean_dot)
    return (grad_in, jnp.sum(grad_rows * unit_rows, axis=0), jnp.sum(grad_rows, axis=0))


def gelu_exact(arg_values):
    return 0.5 * arg_values * (1.0 + jax.scipy.special.erf(arg_values * inv_root_two))


def gelu_slope(arg_values):
    return (
        0.5 * (1.0 + jax.scipy.special.erf(arg_values * inv_root_two))
        + arg_values * jnp.exp(-0.5 * arg_values * arg_values) * inv_root_two_pi
    )


def attend_forward(packed_heads):
    queries = packed_heads[:, :, 0]
    key_rows = packed_heads[:, :, 1]
    values = packed_heads[:, :, 2]
    router_scores = jnp.einsum(
        "ishd,ithd->ihst", queries, key_rows, preferred_element_type=jnp.float32
    ) * HEAD ** (-0.5)
    log_total = jnp.log(jnp.sum(jnp.exp(router_scores), axis=-1, keepdims=True))
    weights = jnp.exp(router_scores - log_total).astype(jnp.bfloat16)
    mixed_heads = jnp.einsum("ihst,ithd->ishd", weights, values, preferred_element_type=jnp.float32)
    return (mixed_heads.astype(jnp.bfloat16), log_total)


def attend_back(packed_heads, log_total, grad_mixed):
    queries = packed_heads[:, :, 0]
    key_rows = packed_heads[:, :, 1]
    values = packed_heads[:, :, 2]
    router_scores = jnp.einsum(
        "ishd,ithd->ihst", queries, key_rows, preferred_element_type=jnp.float32
    ) * HEAD ** (-0.5)
    weights = jnp.exp(router_scores - log_total)
    rounded = weights.astype(jnp.bfloat16)
    grad_values = jnp.einsum(
        "ihst,ishd->ithd", rounded, grad_mixed, preferred_element_type=jnp.float32
    )
    grad_weights = jnp.einsum(
        "ishd,ithd->ihst", grad_mixed, values, preferred_element_type=jnp.float32
    )
    row_delta = jnp.sum(weights * grad_weights, axis=-1, keepdims=True)
    grad_scores = (weights * (grad_weights - row_delta) * HEAD ** (-0.5)).astype(jnp.bfloat16)
    grad_queries = jnp.einsum(
        "ihst,ithd->ishd", grad_scores, key_rows, preferred_element_type=jnp.float32
    )
    grad_keys = jnp.einsum(
        "ihst,ishd->ithd", grad_scores, queries, preferred_element_type=jnp.float32
    )
    return jnp.stack([grad_queries, grad_keys, grad_values], axis=2)


WIDE_EXTRA = 128


def gather_dense(parts):
    joined = jnp.concatenate(parts, axis=1)
    joined = jnp.pad(joined, ((0, 0), (0, -joined.shape[1] % WIDE_EXTRA)))
    return lax.all_gather(joined, ("dp", "expert"), axis=0, tiled=True)


def scatter_dense(parts):
    joined = jnp.concatenate([part.astype(jnp.bfloat16) for part in parts], axis=1)
    joined = jnp.pad(joined, ((0, 0), (0, -joined.shape[1] % WIDE_EXTRA)))
    return lax.psum_scatter(joined, ("dp", "expert"), scatter_dimension=0, tiled=True)


def per_device(
    tokens,
    packed_weight,
    output_weight,
    router_weight,
    first_gain,
    first_bias,
    second_gain,
    second_bias,
    expert_up,
    expert_down,
    expert_choice,
    slot_index,
    cotangent,
):
    local_tokens = tokens.shape[0]
    model_width = tokens.shape[1]
    top_count = expert_choice.shape[1]
    experts = lax.axis_size("expert")
    capacity = max(15 * local_tokens * top_count // (16 * experts), 2)
    dense = gather_dense(
        [
            packed_weight,
            output_weight,
            router_weight,
            first_gain[:, None],
            first_bias[:, None],
            second_gain[:, None],
            second_bias[:, None],
        ]
    )
    packed_full = dense[:, : 3 * model_width]
    output_full = dense[:, 3 * model_width : 4 * model_width]
    router_full = dense[:, 4 * model_width : 4 * model_width + experts]
    vectors = dense[:, 4 * model_width + experts : 4 * model_width + experts + 4].T
    gain_first, bias_first, second_norm_gain, bias_second = (vectors[i] for i in range(4))
    projections = lax.all_gather(
        jnp.concatenate([expert_up, expert_down], axis=0), "dp", axis=0, tiled=False
    )
    weight_up = projections[:, 0]
    weight_down = projections[:, 1]
    inputs = tokens.astype(jnp.float32)
    normed_first, unit_first, inverse_first = normalize(inputs, gain_first, bias_first)
    normed_first = normed_first.astype(jnp.bfloat16)
    packed = jnp.dot(normed_first, packed_full, preferred_element_type=jnp.float32).astype(
        jnp.bfloat16
    )
    packed_heads = packed.reshape(local_tokens // SEQ, SEQ, 3, HEADS, HEAD)
    mixed_heads, log_total = attend_forward(packed_heads)
    mixed_flat = mixed_heads.reshape(local_tokens, model_width)
    hidden_first = inputs + jnp.dot(mixed_flat, output_full, preferred_element_type=jnp.float32)
    normed_second, unit_second, inverse_second = normalize(
        hidden_first, second_norm_gain, bias_second
    )
    normed_second = normed_second.astype(jnp.bfloat16)
    logits = jnp.dot(normed_second, router_full, preferred_element_type=jnp.float32)
    exp_terms = jnp.exp(logits)
    router_probs = exp_terms / jnp.sum(exp_terms, axis=-1, keepdims=True)
    labels = jnp.arange(experts, dtype=jnp.int32)
    choice_mask = (expert_choice[:, :, None] == labels[None, None, :]).astype(jnp.float32)
    gate_values = jnp.sum(choice_mask * router_probs[:, None, :], axis=2)
    local_slot = jnp.where(
        slot_index < capacity, expert_choice * capacity + slot_index, experts * capacity
    ).reshape(-1)

    grad_top = cotangent.astype(jnp.float32)
    slots = jnp.arange(experts * capacity, dtype=jnp.int32)
    local_slot = local_slot.reshape(local_tokens, top_count)
    place = [
        (local_slot[:, k, None] == slots[None, :]).astype(jnp.bfloat16) for k in range(top_count)
    ]
    place_any = sum(place[1:], place[0])
    slot_gate = sum(
        jnp.sum(place[k].astype(jnp.float32) * gate_values[:, k, None], axis=0)
        for k in range(top_count)
    )
    sent = lax.dot_general(
        place_any,
        jnp.concatenate([normed_second, cotangent], axis=1),
        (((0,), (0,)), ((), ())),
        preferred_element_type=jnp.float32,
    )
    sent = jnp.stack(
        [
            sent[:, :model_width].astype(jnp.bfloat16).reshape(experts, capacity, model_width),
            (sent[:, model_width:] * slot_gate[:, None])
            .astype(jnp.bfloat16)
            .reshape(experts, capacity, model_width),
        ],
        axis=1,
    )
    landed = lax.all_to_all(sent, "expert", split_axis=0, concat_axis=0, tiled=True)
    arrived = landed[:, 0].reshape(experts * capacity, model_width)
    grad_arrived = landed[:, 1].reshape(experts * capacity, model_width)
    before_act = jnp.einsum("rd,pdf->prf", arrived, weight_up, preferred_element_type=jnp.float32)
    grad_hidden_act = jnp.einsum(
        "rd,pdf->prf", grad_arrived, weight_down, preferred_element_type=jnp.float32
    )
    hidden = gelu_exact(before_act).astype(jnp.bfloat16)
    grad_pre = (grad_hidden_act * gelu_slope(before_act)).astype(jnp.bfloat16)
    produced = jnp.einsum(
        "prf,pdf->rd", hidden, weight_down, preferred_element_type=jnp.float32
    ).astype(jnp.bfloat16)
    grad_sent = jnp.einsum(
        "prf,pdf->rd", grad_pre, weight_up, preferred_element_type=jnp.float32
    ).astype(jnp.bfloat16)
    came_back = lax.all_to_all(
        jnp.stack(
            [
                produced.reshape(experts, capacity, model_width),
                grad_sent.reshape(experts, capacity, model_width),
            ],
            axis=1,
        ),
        "expert",
        split_axis=0,
        concat_axis=0,
        tiled=True,
    )
    grad_down_full = jnp.einsum(
        "rd,prf->pdf", grad_arrived, hidden, preferred_element_type=jnp.float32
    )
    grad_up_full = jnp.einsum("rd,prf->pdf", arrived, grad_pre, preferred_element_type=jnp.float32)
    expert_grads = lax.psum_scatter(
        jnp.concatenate(
            [grad_up_full.astype(jnp.bfloat16), grad_down_full.astype(jnp.bfloat16)], axis=1
        ).reshape(-1, grad_up_full.shape[2]),
        "dp",
        scatter_dimension=0,
        tiled=True,
    ).astype(jnp.float32)
    expert_grads = expert_grads.reshape(2, model_width, grad_up_full.shape[2])
    grad_up_part, grad_down_part = expert_grads[0], expert_grads[1]
    returned_rows = came_back[:, 0].reshape(experts * capacity, model_width)
    grad_back = came_back[:, 1].reshape(experts * capacity, model_width)
    returned = [
        jnp.dot(place[k], returned_rows, preferred_element_type=jnp.float32)
        for k in range(top_count)
    ]
    combined = sum(gate_values[:, k, None] * returned[k] for k in range(top_count))
    block_output = (hidden_first + combined).astype(jnp.bfloat16)
    grad_gates = jnp.stack(
        [jnp.sum(grad_top * returned[k], axis=1) for k in range(top_count)], axis=1
    )
    gradient_second_normed = jnp.dot(place_any, grad_back, preferred_element_type=jnp.float32)
    grad_probs = jnp.sum(choice_mask * grad_gates[:, :, None], axis=1)
    grad_logits = (
        router_probs * (grad_probs - jnp.sum(router_probs * grad_probs, axis=1, keepdims=True))
    ).astype(jnp.bfloat16)
    grad_router = jnp.dot(normed_second.T, grad_logits, preferred_element_type=jnp.float32)
    gradient_second_normed = gradient_second_normed + jnp.einsum(
        "te,de->td", grad_logits, router_full, preferred_element_type=jnp.float32
    )
    grad_hidden, grad_gain_second, grad_bias_second = normalize_back(
        gradient_second_normed, unit_second, inverse_second, second_norm_gain
    )
    grad_hidden = grad_hidden + grad_top
    grad_hidden_half = grad_hidden.astype(jnp.bfloat16)
    grad_output = jnp.dot(mixed_flat.T, grad_hidden_half, preferred_element_type=jnp.float32)
    grad_mixed = jnp.einsum(
        "td,ed->te", grad_hidden_half, output_full, preferred_element_type=jnp.float32
    ).astype(jnp.bfloat16)
    grad_mixed = grad_mixed.reshape(local_tokens // SEQ, SEQ, HEADS, HEAD)
    gradient_packed_rows = (
        attend_back(packed_heads, log_total, grad_mixed)
        .reshape(local_tokens, 3 * model_width)
        .astype(jnp.bfloat16)
    )
    grad_packed_weight = jnp.dot(
        normed_first.T, gradient_packed_rows, preferred_element_type=jnp.float32
    )
    grad_normed_first = jnp.einsum(
        "tc,dc->td", gradient_packed_rows, packed_full, preferred_element_type=jnp.float32
    )
    grad_inputs, grad_gain_first, grad_bias_first = normalize_back(
        grad_normed_first, unit_first, inverse_first, gain_first
    )
    input_grad = (grad_inputs + grad_hidden).astype(jnp.bfloat16)
    owned = scatter_dense(
        [
            grad_packed_weight,
            grad_output,
            grad_router,
            jnp.stack([grad_gain_first, grad_bias_first, grad_gain_second, grad_bias_second]).T,
        ]
    ).astype(jnp.float32)
    extra = 4 * model_width + experts
    return (
        block_output,
        input_grad,
        owned[:, : 3 * model_width],
        owned[:, 3 * model_width : 4 * model_width],
        owned[:, 4 * model_width : extra],
        owned[:, extra],
        owned[:, extra + 1],
        owned[:, extra + 2],
        owned[:, extra + 3],
        grad_up_part[None],
        grad_down_part[None],
    )


def solution(mesh):
    return jax.shard_map(
        per_device,
        mesh=mesh,
        in_specs=(
            P(("dp", "expert"), None),
            P(("dp", "expert"), None),
            P(("dp", "expert"), None),
            P(("dp", "expert"), None),
            P(("dp", "expert")),
            P(("dp", "expert")),
            P(("dp", "expert")),
            P(("dp", "expert")),
            P("expert", None, "dp"),
            P("expert", None, "dp"),
            P(("dp", "expert"), None),
            P(("dp", "expert"), None),
            P(("dp", "expert"), None),
        ),
        out_specs=(
            P(("dp", "expert"), None),
            P(("dp", "expert"), None),
            P(("dp", "expert"), None),
            P(("dp", "expert"), None),
            P(("dp", "expert"), None),
            P(("dp", "expert")),
            P(("dp", "expert")),
            P(("dp", "expert")),
            P(("dp", "expert")),
            P("expert", None, "dp"),
            P("expert", None, "dp"),
        ),
        check_vma=False,
    )
```

```python
import jax
import jax.numpy as jnp
from jax import lax
from jax.sharding import PartitionSpec as P

HEADS = 12
HEAD = 64
SEQ = 197


epsilon = 1e-06
inv_root_two = 0.7071067811865476
inv_root_two_pi = 0.3989422804014327


def normalize(rows_in, gain_vec, offset):
    centred = rows_in - jnp.mean(rows_in, axis=-1, keepdims=True)
    inverse = lax.rsqrt(jnp.mean(centred * centred, axis=-1, keepdims=True) + epsilon)
    unit_rows = centred * inverse
    return (
        unit_rows * gain_vec.astype(jnp.float32) + offset.astype(jnp.float32),
        unit_rows,
        inverse,
    )


def normalize_back(grad_rows, unit_rows, inverse, gain_vec):
    grad_unit = grad_rows * gain_vec.astype(jnp.float32)
    mean_grad = jnp.mean(grad_unit, axis=-1, keepdims=True)
    mean_dot = jnp.mean(grad_unit * unit_rows, axis=-1, keepdims=True)
    grad_in = inverse * (grad_unit - mean_grad - unit_rows * mean_dot)
    return (grad_in, jnp.sum(grad_rows * unit_rows, axis=0), jnp.sum(grad_rows, axis=0))


def gelu_exact(arg_values):
    return 0.5 * arg_values * (1.0 + jax.scipy.special.erf(arg_values * inv_root_two))


def gelu_slope(arg_values):
    return (
        0.5 * (1.0 + jax.scipy.special.erf(arg_values * inv_root_two))
        + arg_values * jnp.exp(-0.5 * arg_values * arg_values) * inv_root_two_pi
    )


def attend_forward(packed_heads):
    queries = packed_heads[:, :, 0]
    key_rows = packed_heads[:, :, 1]
    values = packed_heads[:, :, 2]
    router_scores = jnp.einsum(
        "ishd,ithd->ihst", queries, key_rows, preferred_element_type=jnp.float32
    ) * HEAD ** (-0.5)
    log_total = jnp.log(jnp.sum(jnp.exp(router_scores), axis=-1, keepdims=True))
    weights = jnp.exp(router_scores - log_total).astype(jnp.bfloat16)
    mixed_heads = jnp.einsum("ihst,ithd->ishd", weights, values, preferred_element_type=jnp.float32)
    return (mixed_heads.astype(jnp.bfloat16), log_total)


def attend_back(packed_heads, log_total, grad_mixed):
    queries = packed_heads[:, :, 0]
    key_rows = packed_heads[:, :, 1]
    values = packed_heads[:, :, 2]
    router_scores = jnp.einsum(
        "ishd,ithd->ihst", queries, key_rows, preferred_element_type=jnp.float32
    ) * HEAD ** (-0.5)
    weights = jnp.exp(router_scores - log_total)
    rounded = weights.astype(jnp.bfloat16)
    grad_values = jnp.einsum(
        "ihst,ishd->ithd", rounded, grad_mixed, preferred_element_type=jnp.float32
    )
    grad_weights = jnp.einsum(
        "ishd,ithd->ihst", grad_mixed, values, preferred_element_type=jnp.float32
    )
    row_delta = jnp.sum(weights * grad_weights, axis=-1, keepdims=True)
    grad_scores = (weights * (grad_weights - row_delta) * HEAD ** (-0.5)).astype(jnp.bfloat16)
    grad_queries = jnp.einsum(
        "ihst,ithd->ishd", grad_scores, key_rows, preferred_element_type=jnp.float32
    )
    grad_keys = jnp.einsum(
        "ihst,ishd->ithd", grad_scores, queries, preferred_element_type=jnp.float32
    )
    return jnp.stack([grad_queries, grad_keys, grad_values], axis=2)


WIDE_EXTRA = 128


def gather_dense(parts):
    joined = jnp.concatenate(parts, axis=1)
    joined = jnp.pad(joined, ((0, 0), (0, -joined.shape[1] % WIDE_EXTRA)))
    return lax.all_gather(joined, ("dp", "expert"), axis=0, tiled=True)


def join_dense(parts):
    joined = jnp.concatenate([part.astype(jnp.bfloat16) for part in parts], axis=1)
    return jnp.pad(joined, ((0, 0), (0, -joined.shape[1] % WIDE_EXTRA)))


def per_device(
    tokens,
    packed_weight,
    output_weight,
    router_weight,
    first_gain,
    first_bias,
    second_gain,
    second_bias,
    expert_up,
    expert_down,
    expert_choice,
    slot_index,
    cotangent,
):
    local_tokens = tokens.shape[0]
    model_width = tokens.shape[1]
    top_count = expert_choice.shape[1]
    experts = lax.axis_size("expert")
    capacity = max(15 * local_tokens * top_count // (16 * experts), 2)
    dense = gather_dense(
        [
            packed_weight,
            output_weight,
            router_weight,
            first_gain[:, None],
            first_bias[:, None],
            second_gain[:, None],
            second_bias[:, None],
        ]
    )
    packed_full = dense[:, : 3 * model_width]
    output_full = dense[:, 3 * model_width : 4 * model_width]
    router_full = dense[:, 4 * model_width : 4 * model_width + experts]
    vectors = dense[:, 4 * model_width + experts : 4 * model_width + experts + 4].T
    gain_first, bias_first, second_norm_gain, bias_second = (vectors[i] for i in range(4))
    projections = lax.all_gather(
        jnp.concatenate([expert_up, expert_down], axis=0), "dp", axis=0, tiled=False
    )
    weight_up = projections[:, 0]
    weight_down = projections[:, 1]
    inputs = tokens.astype(jnp.float32)
    normed_first, unit_first, inverse_first = normalize(inputs, gain_first, bias_first)
    normed_first = normed_first.astype(jnp.bfloat16)
    packed = jnp.dot(normed_first, packed_full, preferred_element_type=jnp.float32).astype(
        jnp.bfloat16
    )
    packed_heads = packed.reshape(local_tokens // SEQ, SEQ, 3, HEADS, HEAD)
    mixed_heads, log_total = attend_forward(packed_heads)
    mixed_flat = mixed_heads.reshape(local_tokens, model_width)
    hidden_first = inputs + jnp.dot(mixed_flat, output_full, preferred_element_type=jnp.float32)
    normed_second, unit_second, inverse_second = normalize(
        hidden_first, second_norm_gain, bias_second
    )
    normed_second = normed_second.astype(jnp.bfloat16)
    logits = jnp.dot(normed_second, router_full, preferred_element_type=jnp.float32)
    exp_terms = jnp.exp(logits)
    router_probs = exp_terms / jnp.sum(exp_terms, axis=-1, keepdims=True)
    labels = jnp.arange(experts, dtype=jnp.int32)
    choice_mask = (expert_choice[:, :, None] == labels[None, None, :]).astype(jnp.float32)
    gate_values = jnp.sum(choice_mask * router_probs[:, None, :], axis=2)
    local_slot = jnp.where(
        slot_index < capacity, expert_choice * capacity + slot_index, experts * capacity
    ).reshape(-1)

    grad_top = cotangent.astype(jnp.float32)
    slots = jnp.arange(experts * capacity, dtype=jnp.int32)
    local_slot = local_slot.reshape(local_tokens, top_count)
    place = [
        (local_slot[:, k, None] == slots[None, :]).astype(jnp.bfloat16) for k in range(top_count)
    ]
    place_any = sum(place[1:], place[0])
    slot_gate = sum(
        jnp.sum(place[k].astype(jnp.float32) * gate_values[:, k, None], axis=0)
        for k in range(top_count)
    )
    sent = lax.dot_general(
        place_any,
        jnp.concatenate([normed_second, cotangent], axis=1),
        (((0,), (0,)), ((), ())),
        preferred_element_type=jnp.float32,
    )
    sent = jnp.stack(
        [
            sent[:, :model_width].astype(jnp.bfloat16).reshape(experts, capacity, model_width),
            (sent[:, model_width:] * slot_gate[:, None])
            .astype(jnp.bfloat16)
            .reshape(experts, capacity, model_width),
        ],
        axis=1,
    )
    landed = lax.all_to_all(sent, "expert", split_axis=0, concat_axis=0, tiled=True)
    arrived = landed[:, 0].reshape(experts * capacity, model_width)
    grad_arrived = landed[:, 1].reshape(experts * capacity, model_width)
    before_act = jnp.einsum("rd,pdf->prf", arrived, weight_up, preferred_element_type=jnp.float32)
    grad_hidden_act = jnp.einsum(
        "rd,pdf->prf", grad_arrived, weight_down, preferred_element_type=jnp.float32
    )
    hidden = gelu_exact(before_act).astype(jnp.bfloat16)
    grad_pre = (grad_hidden_act * gelu_slope(before_act)).astype(jnp.bfloat16)
    produced = jnp.einsum(
        "prf,pdf->rd", hidden, weight_down, preferred_element_type=jnp.float32
    ).astype(jnp.bfloat16)
    grad_sent = jnp.einsum(
        "prf,pdf->rd", grad_pre, weight_up, preferred_element_type=jnp.float32
    ).astype(jnp.bfloat16)
    came_back = lax.all_to_all(
        jnp.stack(
            [
                produced.reshape(experts, capacity, model_width),
                grad_sent.reshape(experts, capacity, model_width),
            ],
            axis=1,
        ),
        "expert",
        split_axis=0,
        concat_axis=0,
        tiled=True,
    )
    grad_down_full = jnp.einsum(
        "rd,prf->pdf", grad_arrived, hidden, preferred_element_type=jnp.float32
    )
    grad_up_full = jnp.einsum("rd,prf->pdf", arrived, grad_pre, preferred_element_type=jnp.float32)
    expert_joined = jnp.concatenate(
        [grad_up_full.astype(jnp.bfloat16), grad_down_full.astype(jnp.bfloat16)], axis=1
    ).reshape(-1, grad_up_full.shape[2])
    expert_joined, came_back = lax.optimization_barrier((expert_joined, came_back))
    expert_grads = lax.psum_scatter(expert_joined, "dp", scatter_dimension=0, tiled=True)
    expert_grads = expert_grads.reshape(2, model_width, grad_up_full.shape[2])
    returned_rows = came_back[:, 0].reshape(experts * capacity, model_width)
    grad_back = came_back[:, 1].reshape(experts * capacity, model_width)
    returned = [
        jnp.dot(place[k], returned_rows, preferred_element_type=jnp.float32)
        for k in range(top_count)
    ]
    combined = sum(gate_values[:, k, None] * returned[k] for k in range(top_count))
    block_output = (hidden_first + combined).astype(jnp.bfloat16)
    grad_gates = jnp.stack(
        [jnp.sum(grad_top * returned[k], axis=1) for k in range(top_count)], axis=1
    )
    gradient_second_normed = jnp.dot(place_any, grad_back, preferred_element_type=jnp.float32)
    grad_probs = jnp.sum(choice_mask * grad_gates[:, :, None], axis=1)
    grad_logits = (
        router_probs * (grad_probs - jnp.sum(router_probs * grad_probs, axis=1, keepdims=True))
    ).astype(jnp.bfloat16)
    grad_router = jnp.dot(normed_second.T, grad_logits, preferred_element_type=jnp.float32)
    gradient_second_normed = gradient_second_normed + jnp.einsum(
        "te,de->td", grad_logits, router_full, preferred_element_type=jnp.float32
    )
    grad_hidden, grad_gain_second, grad_bias_second = normalize_back(
        gradient_second_normed, unit_second, inverse_second, second_norm_gain
    )
    grad_hidden = grad_hidden + grad_top
    grad_hidden_half = grad_hidden.astype(jnp.bfloat16)
    grad_output = jnp.dot(mixed_flat.T, grad_hidden_half, preferred_element_type=jnp.float32)
    grad_mixed = jnp.einsum(
        "td,ed->te", grad_hidden_half, output_full, preferred_element_type=jnp.float32
    ).astype(jnp.bfloat16)
    grad_mixed = grad_mixed.reshape(local_tokens // SEQ, SEQ, HEADS, HEAD)
    gradient_packed_rows = (
        attend_back(packed_heads, log_total, grad_mixed)
        .reshape(local_tokens, 3 * model_width)
        .astype(jnp.bfloat16)
    )
    grad_packed_weight = jnp.dot(
        normed_first.T, gradient_packed_rows, preferred_element_type=jnp.float32
    )
    grad_normed_first = jnp.einsum(
        "tc,dc->td", gradient_packed_rows, packed_full, preferred_element_type=jnp.float32
    )
    grad_inputs, grad_gain_first, grad_bias_first = normalize_back(
        grad_normed_first, unit_first, inverse_first, gain_first
    )
    input_grad = (grad_inputs + grad_hidden).astype(jnp.bfloat16)
    dense_joined = join_dense(
        [
            grad_packed_weight,
            grad_output,
            grad_router,
            jnp.stack([grad_gain_first, grad_bias_first, grad_gain_second, grad_bias_second]).T,
        ]
    )
    dense_joined, expert_grads = lax.optimization_barrier((dense_joined, expert_grads))
    owned = lax.psum_scatter(
        dense_joined, ("dp", "expert"), scatter_dimension=0, tiled=True
    ).astype(jnp.float32)
    grad_up_part, grad_down_part = (expert_grads[i].astype(jnp.float32) for i in range(2))
    extra = 4 * model_width + experts
    return (
        block_output,
        input_grad,
        owned[:, : 3 * model_width],
        owned[:, 3 * model_width : 4 * model_width],
        owned[:, 4 * model_width : extra],
        owned[:, extra],
        owned[:, extra + 1],
        owned[:, extra + 2],
        owned[:, extra + 3],
        grad_up_part[None],
        grad_down_part[None],
    )


def solution(mesh):
    return jax.shard_map(
        per_device,
        mesh=mesh,
        in_specs=(
            P(("dp", "expert"), None),
            P(("dp", "expert"), None),
            P(("dp", "expert"), None),
            P(("dp", "expert"), None),
            P(("dp", "expert")),
            P(("dp", "expert")),
            P(("dp", "expert")),
            P(("dp", "expert")),
            P("expert", None, "dp"),
            P("expert", None, "dp"),
            P(("dp", "expert"), None),
            P(("dp", "expert"), None),
            P(("dp", "expert"), None),
        ),
        out_specs=(
            P(("dp", "expert"), None),
            P(("dp", "expert"), None),
            P(("dp", "expert"), None),
            P(("dp", "expert"), None),
            P(("dp", "expert"), None),
            P(("dp", "expert")),
            P(("dp", "expert")),
            P(("dp", "expert")),
            P(("dp", "expert")),
            P("expert", None, "dp"),
            P("expert", None, "dp"),
        ),
        check_vma=False,
    )
```

```python
import jax
import jax.numpy as jnp
from jax import lax
from jax.sharding import PartitionSpec as P

HEADS = 12
HEAD = 64
SEQ = 197


epsilon = 1e-06
inv_root_two = 0.7071067811865476
inv_root_two_pi = 0.3989422804014327


def normalize(rows_in, gain_vec, offset):
    centred = rows_in - jnp.mean(rows_in, axis=-1, keepdims=True)
    inverse = lax.rsqrt(jnp.mean(centred * centred, axis=-1, keepdims=True) + epsilon)
    unit_rows = centred * inverse
    return (
        unit_rows * gain_vec.astype(jnp.float32) + offset.astype(jnp.float32),
        unit_rows,
        inverse,
    )


def normalize_back(grad_rows, unit_rows, inverse, gain_vec):
    grad_unit = grad_rows * gain_vec.astype(jnp.float32)
    mean_grad = jnp.mean(grad_unit, axis=-1, keepdims=True)
    mean_dot = jnp.mean(grad_unit * unit_rows, axis=-1, keepdims=True)
    grad_in = inverse * (grad_unit - mean_grad - unit_rows * mean_dot)
    return (grad_in, jnp.sum(grad_rows * unit_rows, axis=0), jnp.sum(grad_rows, axis=0))


def gelu_exact(arg_values):
    return 0.5 * arg_values * (1.0 + jax.scipy.special.erf(arg_values * inv_root_two))


def gelu_slope(arg_values):
    return (
        0.5 * (1.0 + jax.scipy.special.erf(arg_values * inv_root_two))
        + arg_values * jnp.exp(-0.5 * arg_values * arg_values) * inv_root_two_pi
    )


def attend_forward(packed_heads):
    queries = packed_heads[:, :, 0]
    key_rows = packed_heads[:, :, 1]
    values = packed_heads[:, :, 2]
    router_scores = jnp.einsum(
        "ishd,ithd->ihst", queries, key_rows, preferred_element_type=jnp.float32
    ) * HEAD ** (-0.5)
    log_total = jnp.log(jnp.sum(jnp.exp(router_scores), axis=-1, keepdims=True))
    weights = jnp.exp(router_scores - log_total).astype(jnp.bfloat16)
    mixed_heads = jnp.einsum("ihst,ithd->ishd", weights, values, preferred_element_type=jnp.float32)
    return (mixed_heads.astype(jnp.bfloat16), log_total)


def attend_back(packed_heads, log_total, grad_mixed):
    queries = packed_heads[:, :, 0]
    key_rows = packed_heads[:, :, 1]
    values = packed_heads[:, :, 2]
    router_scores = jnp.einsum(
        "ishd,ithd->ihst", queries, key_rows, preferred_element_type=jnp.float32
    ) * HEAD ** (-0.5)
    weights = jnp.exp(router_scores - log_total)
    rounded = weights.astype(jnp.bfloat16)
    grad_values = jnp.einsum(
        "ihst,ishd->ithd", rounded, grad_mixed, preferred_element_type=jnp.float32
    )
    grad_weights = jnp.einsum(
        "ishd,ithd->ihst", grad_mixed, values, preferred_element_type=jnp.float32
    )
    row_delta = jnp.sum(weights * grad_weights, axis=-1, keepdims=True)
    grad_scores = (weights * (grad_weights - row_delta) * HEAD ** (-0.5)).astype(jnp.bfloat16)
    grad_queries = jnp.einsum(
        "ihst,ithd->ishd", grad_scores, key_rows, preferred_element_type=jnp.float32
    )
    grad_keys = jnp.einsum(
        "ihst,ishd->ithd", grad_scores, queries, preferred_element_type=jnp.float32
    )
    return jnp.stack([grad_queries, grad_keys, grad_values], axis=2)


WIDE_EXTRA = 128


def gather_dense(parts):
    joined = jnp.concatenate(parts, axis=1)
    joined = jnp.pad(joined, ((0, 0), (0, -joined.shape[1] % WIDE_EXTRA)))
    return lax.all_gather(joined, ("dp", "expert"), axis=0, tiled=True)


def join_dense(parts):
    width = sum(part.shape[1] for part in parts)
    filler = jnp.zeros((parts[0].shape[0], -width % WIDE_EXTRA), jnp.bfloat16)
    return jnp.concatenate([part.astype(jnp.bfloat16) for part in parts] + [filler], axis=1)


def per_device(
    tokens,
    packed_weight,
    output_weight,
    router_weight,
    first_gain,
    first_bias,
    second_gain,
    second_bias,
    expert_up,
    expert_down,
    expert_choice,
    slot_index,
    cotangent,
):
    local_tokens = tokens.shape[0]
    model_width = tokens.shape[1]
    top_count = expert_choice.shape[1]
    experts = lax.axis_size("expert")
    capacity = max(15 * local_tokens * top_count // (16 * experts), 2)
    dense = gather_dense(
        [
            packed_weight,
            output_weight,
            router_weight,
            first_gain[:, None],
            first_bias[:, None],
            second_gain[:, None],
            second_bias[:, None],
        ]
    )
    packed_full = dense[:, : 3 * model_width]
    output_full = dense[:, 3 * model_width : 4 * model_width]
    router_full = dense[:, 4 * model_width : 4 * model_width + experts]
    vectors = dense[:, 4 * model_width + experts : 4 * model_width + experts + 4].T
    gain_first, bias_first, second_norm_gain, bias_second = (vectors[i] for i in range(4))
    projections = lax.all_gather(
        jnp.concatenate([expert_up, expert_down], axis=0), "dp", axis=0, tiled=False
    )
    weight_up = projections[:, 0]
    weight_down = projections[:, 1]
    inputs = tokens.astype(jnp.float32)
    normed_first, unit_first, inverse_first = normalize(inputs, gain_first, bias_first)
    normed_first = normed_first.astype(jnp.bfloat16)
    packed = jnp.dot(normed_first, packed_full, preferred_element_type=jnp.float32).astype(
        jnp.bfloat16
    )
    packed_heads = packed.reshape(local_tokens // SEQ, SEQ, 3, HEADS, HEAD)
    mixed_heads, log_total = attend_forward(packed_heads)
    mixed_flat = mixed_heads.reshape(local_tokens, model_width)
    hidden_first = inputs + jnp.dot(mixed_flat, output_full, preferred_element_type=jnp.float32)
    normed_second, unit_second, inverse_second = normalize(
        hidden_first, second_norm_gain, bias_second
    )
    normed_second = normed_second.astype(jnp.bfloat16)
    logits = jnp.dot(normed_second, router_full, preferred_element_type=jnp.float32)
    exp_terms = jnp.exp(logits)
    router_probs = exp_terms / jnp.sum(exp_terms, axis=-1, keepdims=True)
    labels = jnp.arange(experts, dtype=jnp.int32)
    choice_mask = (expert_choice[:, :, None] == labels[None, None, :]).astype(jnp.float32)
    gate_values = jnp.sum(choice_mask * router_probs[:, None, :], axis=2)
    local_slot = jnp.where(
        slot_index < capacity, expert_choice * capacity + slot_index, experts * capacity
    ).reshape(-1)

    grad_top = cotangent.astype(jnp.float32)
    slots = jnp.arange(experts * capacity, dtype=jnp.int32)
    local_slot = local_slot.reshape(local_tokens, top_count)
    place = [
        (local_slot[:, k, None] == slots[None, :]).astype(jnp.bfloat16) for k in range(top_count)
    ]
    place_any = sum(place[1:], place[0])
    slot_gate = sum(
        jnp.sum(place[k].astype(jnp.float32) * gate_values[:, k, None], axis=0)
        for k in range(top_count)
    )
    sent = lax.dot_general(
        place_any,
        jnp.concatenate([normed_second, cotangent], axis=1),
        (((0,), (0,)), ((), ())),
        preferred_element_type=jnp.float32,
    )
    sent = jnp.stack(
        [
            sent[:, :model_width].astype(jnp.bfloat16).reshape(experts, capacity, model_width),
            (sent[:, model_width:] * slot_gate[:, None])
            .astype(jnp.bfloat16)
            .reshape(experts, capacity, model_width),
        ],
        axis=1,
    )
    landed = lax.all_to_all(sent, "expert", split_axis=0, concat_axis=0, tiled=True)
    arrived = landed[:, 0].reshape(experts * capacity, model_width)
    grad_arrived = landed[:, 1].reshape(experts * capacity, model_width)
    before_act = jnp.einsum("rd,pdf->prf", arrived, weight_up, preferred_element_type=jnp.float32)
    grad_hidden_act = jnp.einsum(
        "rd,pdf->prf", grad_arrived, weight_down, preferred_element_type=jnp.float32
    )
    hidden = gelu_exact(before_act).astype(jnp.bfloat16)
    grad_pre = (grad_hidden_act * gelu_slope(before_act)).astype(jnp.bfloat16)
    produced = jnp.einsum(
        "prf,pdf->rd", hidden, weight_down, preferred_element_type=jnp.float32
    ).astype(jnp.bfloat16)
    grad_sent = jnp.einsum(
        "prf,pdf->rd", grad_pre, weight_up, preferred_element_type=jnp.float32
    ).astype(jnp.bfloat16)
    came_back = lax.all_to_all(
        jnp.stack(
            [
                produced.reshape(experts, capacity, model_width),
                grad_sent.reshape(experts, capacity, model_width),
            ],
            axis=1,
        ),
        "expert",
        split_axis=0,
        concat_axis=0,
        tiled=True,
    )
    grad_down_full = jnp.einsum(
        "rd,prf->pdf", grad_arrived, hidden, preferred_element_type=jnp.float32
    )
    grad_up_full = jnp.einsum("rd,prf->pdf", arrived, grad_pre, preferred_element_type=jnp.float32)
    expert_joined = jnp.concatenate(
        [grad_up_full.astype(jnp.bfloat16), grad_down_full.astype(jnp.bfloat16)], axis=1
    ).reshape(-1, grad_up_full.shape[2])
    expert_joined, came_back = lax.optimization_barrier((expert_joined, came_back))
    expert_grads = lax.psum_scatter(expert_joined, "dp", scatter_dimension=0, tiled=True)
    expert_grads = expert_grads.reshape(2, model_width, grad_up_full.shape[2])
    returned_rows = came_back[:, 0].reshape(experts * capacity, model_width)
    grad_back = came_back[:, 1].reshape(experts * capacity, model_width)
    returned = [
        jnp.dot(place[k], returned_rows, preferred_element_type=jnp.float32)
        for k in range(top_count)
    ]
    combined = sum(gate_values[:, k, None] * returned[k] for k in range(top_count))
    block_output = (hidden_first + combined).astype(jnp.bfloat16)
    grad_gates = jnp.stack(
        [jnp.sum(grad_top * returned[k], axis=1) for k in range(top_count)], axis=1
    )
    gradient_second_normed = jnp.dot(place_any, grad_back, preferred_element_type=jnp.float32)
    grad_probs = jnp.sum(choice_mask * grad_gates[:, :, None], axis=1)
    grad_logits = (
        router_probs * (grad_probs - jnp.sum(router_probs * grad_probs, axis=1, keepdims=True))
    ).astype(jnp.bfloat16)
    grad_router = jnp.dot(normed_second.T, grad_logits, preferred_element_type=jnp.float32)
    gradient_second_normed = gradient_second_normed + jnp.einsum(
        "te,de->td", grad_logits, router_full, preferred_element_type=jnp.float32
    )
    grad_hidden, grad_gain_second, grad_bias_second = normalize_back(
        gradient_second_normed, unit_second, inverse_second, second_norm_gain
    )
    grad_hidden = grad_hidden + grad_top
    grad_hidden_half = grad_hidden.astype(jnp.bfloat16)
    grad_output = jnp.dot(mixed_flat.T, grad_hidden_half, preferred_element_type=jnp.float32)
    grad_mixed = jnp.einsum(
        "td,ed->te", grad_hidden_half, output_full, preferred_element_type=jnp.float32
    ).astype(jnp.bfloat16)
    grad_mixed = grad_mixed.reshape(local_tokens // SEQ, SEQ, HEADS, HEAD)
    gradient_packed_rows = (
        attend_back(packed_heads, log_total, grad_mixed)
        .reshape(local_tokens, 3 * model_width)
        .astype(jnp.bfloat16)
    )
    grad_packed_weight = jnp.dot(
        normed_first.T, gradient_packed_rows, preferred_element_type=jnp.float32
    )
    grad_normed_first = jnp.einsum(
        "tc,dc->td", gradient_packed_rows, packed_full, preferred_element_type=jnp.float32
    )
    grad_inputs, grad_gain_first, grad_bias_first = normalize_back(
        grad_normed_first, unit_first, inverse_first, gain_first
    )
    input_grad = (grad_inputs + grad_hidden).astype(jnp.bfloat16)
    dense_joined = join_dense(
        [
            grad_packed_weight,
            grad_output,
            grad_router,
            jnp.stack([grad_gain_first, grad_bias_first, grad_gain_second, grad_bias_second]).T,
        ]
    )
    dense_joined, expert_grads = lax.optimization_barrier((dense_joined, expert_grads))
    owned = lax.psum_scatter(dense_joined, "dp", scatter_dimension=0, tiled=True)
    owned = lax.psum_scatter(owned, "expert", scatter_dimension=0, tiled=True).astype(jnp.float32)
    grad_up_part, grad_down_part = (expert_grads[i].astype(jnp.float32) for i in range(2))
    extra = 4 * model_width + experts
    return (
        block_output,
        input_grad,
        owned[:, : 3 * model_width],
        owned[:, 3 * model_width : 4 * model_width],
        owned[:, 4 * model_width : extra],
        owned[:, extra],
        owned[:, extra + 1],
        owned[:, extra + 2],
        owned[:, extra + 3],
        grad_up_part[None],
        grad_down_part[None],
    )


def solution(mesh):
    return jax.shard_map(
        per_device,
        mesh=mesh,
        in_specs=(
            P(("dp", "expert"), None),
            P(("dp", "expert"), None),
            P(("dp", "expert"), None),
            P(("dp", "expert"), None),
            P(("dp", "expert")),
            P(("dp", "expert")),
            P(("dp", "expert")),
            P(("dp", "expert")),
            P("expert", None, "dp"),
            P("expert", None, "dp"),
            P(("dp", "expert"), None),
            P(("dp", "expert"), None),
            P(("dp", "expert"), None),
        ),
        out_specs=(
            P(("dp", "expert"), None),
            P(("dp", "expert"), None),
            P(("dp", "expert"), None),
            P(("dp", "expert"), None),
            P(("dp", "expert"), None),
            P(("dp", "expert")),
            P(("dp", "expert")),
            P(("dp", "expert")),
            P(("dp", "expert")),
            P("expert", None, "dp"),
            P("expert", None, "dp"),
        ),
        check_vma=False,
    )
```
